512 devices in a mesh: req: 128 (over z_hi, y, x, core), tp: 4 (over z_lo).
Axes of the slice: x: 4, y: 4, z: 16 (z_hi: 4, z_lo: 4; z = z_hi * 4 + z_lo), core: 2. Of those that a mesh axis runs over, the one named last changes fastest.
Arguments:
- queries: bfloat16 [8192, 2560], P('req', 'tp'), may hold values from -20 to 20
- key_values: bfloat16 [8192, 1024], P('req', 'tp'), may hold values from -6 to 6
- hidden: bfloat16 [8192, 2560], P('req'), may hold values from -6 to 6
- lengths: int32 [128, 4], P('req'), may hold values from 1 to 32, 64 in all within a row
- page_table: int32 [128, 4, 2], P('req'), may hold values from 0 to 7, as said below
- out_weight: bfloat16 [2560, 2560], P('tp', 'req'), may hold values from -0.125 to 0.125
- norm_gain: float32 [2560], replicated, may hold values from 0.4 to 1.6
- expert_choice: int32 [8192, 6], P('req'), may hold values from 0 to 63, all different within a row; in each aligned block of 64 rows (0 to 63, 64 to 127, ...) at most 8 rows name the same one
- route_weight: float32 [8192, 6], P('req'), may hold values from 0.05 to 0.5
- gate_up: bfloat16 [128, 2560, 1536], P('req', None, 'tp'), may hold values from -0.125 to 0.125
- down: bfloat16 [128, 768, 2560], P('req', 'tp'), may hold values from -0.15625 to 0.15625
Outputs:
- layer_out: bfloat16 [8192, 2560], P('req', 'tp')
- kv_cache: bfloat16 [1024, 16, 1024], P('req', None, 'tp')
The draws below stay inside these ranges and needn't reach their ends.
Inputs may be any that keep to these rules, and one draw needn't show every extreme that they name: `expert_choice`: among the 64 rows of one index of req no expert is named by more than 8 rows; the 6 experts of a row differ. `page_table`: the 4 x 2 entries of one index of req are its 8 pool pages, each once.
All inputs are finite; a program needn't handle non-finite values.
Results may differ from the reference program's by a relative error of at most 0.0065.
Values may be sent and summed in bfloat16 or wider, within the bound.
No kernel may reach another device: no remote copies, remote signals or barrier semaphores. Data moves between devices by JAX's collectives and lax.ppermute only.
A program may use at most 64 MiB of HBM per device.

```python
import math
import jax
import jax.numpy as jnp
import numpy as np
from jax import lax

D = 2560
HEADS = 20
KV_HEADS = 4
HEAD_DIM = 128
EXPERT_FF = 1536
TOK_DEV = 64
SEGS = 4
PAGE = 16
EXPERTS = 64
TOP = 6
CAP = 8
UNITS = 192
PAGES_SEG = 2
POOL = 8
TOKENS = 8192
N_REQ = 128
N_TP = 4


def attention_fields(key):
    keys = jnp.clip(jax.random.normal(jax.random.fold_in(key, 101), (TOKENS, KV_HEADS, HEAD_DIM), jnp.float32), -6.0, 6.0)
    values = jnp.clip(jax.random.normal(jax.random.fold_in(key, 102), (TOKENS, KV_HEADS, HEAD_DIM), jnp.float32), -6.0, 6.0)
    queries = jnp.clip(jax.random.normal(jax.random.fold_in(key, 103), (TOKENS, HEADS, HEAD_DIM), jnp.float32), -6.0, 6.0)
    return (queries, keys, values)


def draw_queries(key, part):
    queries, keys, values = attention_fields(key)
    return queries.reshape(TOKENS, HEADS * HEAD_DIM).astype(jnp.bfloat16)


def draw_key_values(key, part):
    queries, keys, values = attention_fields(key)
    return jnp.stack([keys, values], axis=2).reshape(TOKENS, KV_HEADS * 2 * HEAD_DIM).astype(jnp.bfloat16)


def permuted_pool(one_key):
    return jax.random.permutation(one_key, POOL)


def draw_page_table(key, part):
    row_keys = jax.random.split(jax.random.fold_in(key, 201), N_REQ)
    orders = jax.vmap(permuted_pool)(row_keys)
    return orders.reshape(N_REQ, SEGS, PAGES_SEG).astype(jnp.int32)


def level_of(key, shape, cuts, least, high):
    def one(dim, blocks):
        draws = jax.random.uniform(jax.random.fold_in(jax.random.fold_in(key, 6), dim), (blocks,), jnp.float32, least / len(cuts), high / len(cuts))
        return jnp.repeat(jnp.exp(draws), shape[dim] // blocks).reshape((-1,) + (1,) * (len(shape) - dim - 1))

    level = one(*cuts[0])
    for cut in cuts[1:]:
        level = level * one(*cut)
    return level


def split_up(amount, total, reach, lean):
    portions = [(1 << 20) // math.isqrt(rank ** lean) + 1 for rank in range(2, amount + 1)]
    surplus, counts = total - reach - (amount - 1), [1] * (amount - 1)
    while surplus > 0:
        candidates = [i for i in range(amount - 1) if counts[i] < reach]
        mass, budget = sum([portions[i] for i in candidates]), surplus
        for i in candidates:
            extra = min(reach - counts[i], max(1, budget * portions[i] // mass), surplus)
            counts[i] = counts[i] + extra
            surplus = surplus - extra
    return np.array([reach] + counts)


def ragged_sizes(rng, number_of, total, reach, slope):
    if number_of == 2:
        one = jax.random.randint(rng, (), max(1, total - reach), min(reach, total - 1) + 1)
        return jnp.stack([one, total - one])
    sizes = jnp.asarray(split_up(number_of, total, reach, slope), jnp.int32)
    pairs = (number_of - 1) // 2
    giver, sink = sizes[1:1 + 2 * pairs:2], sizes[2:2 + 2 * pairs:2]
    room = jnp.minimum(giver - 1, reach - sink)
    shifted = jax.random.randint(jax.random.fold_in(rng, 1), (pairs,), 0, 1 << 20) % (room + 1)
    sizes = sizes.at[1:1 + 2 * pairs:2].set(giver - shifted).at[2:2 + 2 * pairs:2].set(sink + shifted)
    return sizes[jax.random.permutation(jax.random.fold_in(rng, 2), number_of)]


def assign_block(key, own, number, rows, number_of, top, most, skew):
    sequence = jax.random.permutation(key, number_of)
    heavy_load, common = load_shares(number_of, rows * top, most, skew, True), load_shares(number_of, rows * top, most, skew, False)
    places = jnp.arange(number_of)

    def named(tallies, offset_by):
        used = int((tallies > 0).sum())
        fixed = max(1, used // 4)
        passed = fixed + (places - fixed + offset_by * (used - fixed)) % max(1, number_of - fixed)
        return jnp.zeros((number_of,), jnp.int32).at[sequence[jnp.where(places < fixed, places, passed)]].set(jnp.asarray(tallies, jnp.int32))

    tallies = jnp.where(number % 4 == 0, named(heavy_load, number // 4), named(common, number - number // 4 - 1))
    mixed = jax.random.permutation(jax.random.fold_in(own, 3), number_of)
    source_of, taker = mixed[0:number_of // 2 * 2:2], mixed[1:number_of // 2 * 2:2]
    room = jnp.minimum(tallies[source_of] - 1, most - tallies[taker]) // 2
    room = jnp.where((source_of == sequence[0]) | (taker == sequence[0]) | (tallies[taker] == 0), 0, jnp.maximum(room, 0))
    passed = jax.random.randint(jax.random.fold_in(own, 4), (number_of // 2,), 0, 1 << 20) % (room + 1)
    tallies = tallies.at[source_of].add(-passed).at[taker].add(passed)
    members = jnp.searchsorted(jnp.cumsum(tallies), jnp.arange(rows * top), side="right").astype(jnp.int32)
    table = members.reshape(top, rows).T
    table = table[jax.random.permutation(jax.random.fold_in(own, 1), rows)]
    offset_by = jax.random.randint(jax.random.fold_in(own, 2), (rows, 1), 0, top)
    return jnp.take_along_axis(table, (jnp.arange(top)[None, :] + offset_by) % top, axis=1)


def load_shares(amount, total, bound, skew, full):
    loads = [(1 << 20) // math.isqrt(rank ** skew) + 1 for rank in range(1, amount + 1)]
    largest = bound if full else min(bound, max(-(-total // amount), total * loads[0] // sum(loads)))
    least = 1 if total - largest >= amount - 1 else 0
    given, rest = [largest] + [least] * (amount - 1), total - largest - least * (amount - 1)
    while rest > 0:
        movable = [i for i in range(1, amount) if given[i] < largest] or [i for i in range(1, amount) if given[i] < bound]
        pool, left = sum([loads[i] for i in movable]), rest
        for i in movable:
            addition = min(bound - given[i], max(1, left * loads[i] // pool), rest)
            given[i] = given[i] + addition
            rest = rest - addition
    return np.array(given)


def bell_draw(own_key, dims, scale, bound, cuts=(), kind=jnp.bfloat16):
    array = scale * jax.random.normal(own_key, dims, jnp.float32)
    if cuts:
        array = array * level_of(own_key, dims, cuts, -0.22, 0.18)
    return jnp.clip(array, -bound, bound).astype(kind)


def setup_inputs(seed: int = 0) -> dict:
    streams_of = jax.random.split(jax.random.key(seed), 12)
    queries = draw_queries(jax.random.fold_in(streams_of[11], 71), 0)
    key_values = draw_key_values(jax.random.fold_in(streams_of[11], 71), 0)
    hidden = bell_draw(streams_of[2], (TOKENS, D), 1.0, 6.0, ((0, 128),))
    lengths = jax.vmap(lambda own: ragged_sizes(own, SEGS, TOK_DEV, TOK_DEV // 2, 2))(jax.random.split(streams_of[3], N_REQ)).reshape((N_REQ, SEGS)).astype(jnp.int32)
    page_table = draw_page_table(jax.random.fold_in(streams_of[11], 71), 0)
    out_weight = bell_draw(streams_of[5], (HEADS * HEAD_DIM, D), (HEADS * HEAD_DIM) ** -0.5, 0.125, ((0, 4), (1, 128)))
    norm_gain = jnp.clip(jax.random.uniform(streams_of[6], (D,), jnp.float32, 0.4, 1.6), 0.4, 1.6)
    expert_choice_keys = jax.random.split(jax.random.fold_in(streams_of[7], 1), TOKENS // TOK_DEV)
    expert_choice_turns = jax.random.permutation(jax.random.fold_in(streams_of[7], 3), TOKENS // TOK_DEV)
    expert_choice = jax.vmap(lambda own, number: assign_block(jax.random.fold_in(streams_of[7], 2), own, number, TOK_DEV, EXPERTS, TOP, CAP, 2))(expert_choice_keys, expert_choice_turns).reshape((TOKENS, TOP))
    route_weight = jnp.clip(jnp.exp(math.log(0.5) - 2.3025851 * jax.random.uniform(streams_of[8], (TOKENS, TOP), jnp.float32) ** level_of(streams_of[8], (TOKENS, TOP), ((0, 128),), -0.2, 0.2)), 0.05, 0.5)
    gate_up = bell_draw(streams_of[9], (2 * EXPERTS, D, EXPERT_FF), D ** -0.5, 0.125, ((0, 128), (2, 4)))
    down = bell_draw(streams_of[10], (2 * EXPERTS, EXPERT_FF // 2, D), EXPERT_FF ** -0.5, 0.15625, ((0, 128), (1, 4)))
    return dict(queries=queries, key_values=key_values, hidden=hidden, lengths=lengths, page_table=page_table, out_weight=out_weight, norm_gain=norm_gain, expert_choice=expert_choice, route_weight=route_weight, gate_up=gate_up, down=down)


epsilon = 1e-05

def prompt_layout(lengths, count):
    ends = jnp.cumsum(lengths).astype(jnp.int32)
    starts = ends - lengths
    places = jnp.arange(count, dtype=jnp.int32)
    segment = lax.optimization_barrier(jnp.sum((ends[None, :] <= places[:, None]).astype(jnp.int32), axis=1))
    picked = segment[:, None] == jnp.arange(lengths.shape[0], dtype=jnp.int32)[None, :]
    offset = places - lax.optimization_barrier(jnp.sum(jnp.where(picked, starts[None, :], 0), axis=1))
    return (segment, offset)

def attend_block(pieces):
    query_block, key_block, length_row = pieces
    segment, offset = prompt_layout(length_row, TOK_DEV)
    group = HEADS // KV_HEADS
    query_rows = query_block.astype(jnp.float32).reshape(TOK_DEV, KV_HEADS, group, HEAD_DIM)
    key_rows = key_block.astype(jnp.float32).reshape(TOK_DEV, KV_HEADS, 2, HEAD_DIM)
    scores = jnp.einsum('qhgd,khd->hgqk', query_rows, key_rows[:, :, 0]) * HEAD_DIM ** (-0.5)
    places = jnp.arange(TOK_DEV, dtype=jnp.int32)
    allowed = (segment[:, None] == segment[None, :]) & (places[None, :] <= places[:, None])
    scores = jnp.where(allowed[None, None], scores, -1e+30)
    highest = lax.optimization_barrier(jnp.max(scores, axis=-1, keepdims=True))
    weights = jnp.exp(scores - highest)
    probs = (weights / lax.optimization_barrier(jnp.sum(weights, axis=-1, keepdims=True))).astype(jnp.bfloat16)
    context = jnp.einsum('hgqk,khd->qhgd', probs.astype(jnp.float32), key_rows[:, :, 1])
    return context.astype(jnp.bfloat16).reshape(TOK_DEV, HEADS * HEAD_DIM)

def reference(queries, key_values, hidden, lengths, page_table, out_weight, norm_gain, expert_choice, route_weight, gate_up, down):
    context = lax.map(attend_block, (queries.reshape(N_REQ, TOK_DEV, HEADS * HEAD_DIM), key_values.reshape(N_REQ, TOK_DEV, KV_HEADS * 2 * HEAD_DIM), lengths))
    context = context.reshape(TOKENS, HEADS * HEAD_DIM)
    attn = jnp.dot(context, out_weight, preferred_element_type=jnp.float32)
    mid = (hidden.astype(jnp.float32) + attn).astype(jnp.bfloat16)
    mid_wide = lax.optimization_barrier(mid).astype(jnp.float32)
    square = lax.optimization_barrier(jnp.mean(mid_wide * mid_wide, axis=1, keepdims=True))
    normed = (mid_wide * lax.rsqrt(square + epsilon) * norm_gain).astype(jnp.bfloat16)
    chosen = expert_choice.reshape(N_REQ, TOK_DEV * TOP)
    hits = (chosen[:, :, None] == jnp.arange(EXPERTS, dtype=jnp.int32)[None, None, :]).astype(jnp.int32)
    ranks = lax.optimization_barrier(jnp.sum((jnp.cumsum(hits, axis=1) - hits) * hits, axis=2))
    places = (jnp.arange(N_REQ, dtype=jnp.int32)[:, None] * CAP + ranks).reshape(-1).astype(jnp.int32)
    owners = (jnp.arange(TOKENS * TOP, dtype=jnp.int32) // TOP).astype(jnp.int32)
    flat_choice = chosen.reshape(-1)
    flat_weight = route_weight.reshape(-1)
    slots = N_REQ * CAP
    half_units = EXPERT_FF // 2

    def expert_step(total, index):
        valid = flat_choice == index
        where_to = jnp.where(valid, places, slots)
        source = jnp.zeros((slots,), jnp.int32).at[where_to].set(owners, mode='drop')
        weight = jnp.zeros((slots,), jnp.float32).at[where_to].set(flat_weight, mode='drop')
        rows = normed[source].astype(jnp.float32)
        pair_weights = lax.dynamic_slice_in_dim(gate_up, 2 * index, 2, 0).astype(jnp.float32)
        pair_weights = pair_weights.reshape(2, D, N_TP, 2, UNITS)
        gate_weights = pair_weights[:, :, :, 0, :].reshape(2, D, half_units)
        up_weights = pair_weights[:, :, :, 1, :].reshape(2, D, half_units)
        gate = jnp.einsum('nd,hdu->nhu', rows, gate_weights)
        upper = jnp.einsum('nd,hdu->nhu', rows, up_weights)
        activated = (jax.nn.silu(gate) * upper).astype(jnp.bfloat16)
        activated = lax.optimization_barrier(activated).astype(jnp.float32).reshape(slots, 2, N_TP, UNITS)
        pair_down = lax.dynamic_slice_in_dim(down, 2 * index, 2, 0).astype(jnp.float32).reshape(2, N_TP, UNITS, D)
        groups = jnp.einsum('nhtu,htud->nhtd', activated, pair_down).astype(jnp.bfloat16)
        groups = lax.optimization_barrier(groups).astype(jnp.float32)
        result = lax.optimization_barrier(jnp.sum(groups, axis=(1, 2)))
        return (total.at[source].add(result * weight[:, None]), None)
    moe, _ = lax.scan(expert_step, jnp.zeros((TOKENS, D), jnp.float32), jnp.arange(EXPERTS, dtype=jnp.int32))
    layer_out = (mid_wide + moe).astype(jnp.bfloat16)

    def block_rows(length_row, pages):
        segment, offset = prompt_layout(length_row, TOK_DEV)
        flat_pages = pages.reshape(-1)
        page_of = segment * PAGES_SEG + offset // PAGE
        slot_page = lax.optimization_barrier(jnp.sum(jnp.where(page_of[:, None] == jnp.arange(POOL, dtype=jnp.int32)[None, :], flat_pages[None, :], 0), axis=1))
        return (slot_page * PAGE + offset % PAGE).astype(jnp.int32)
    rows = jax.vmap(block_rows)(lengths, page_table) + (jnp.arange(N_REQ, dtype=jnp.int32) * (POOL * PAGE))[:, None]
    cache = jnp.zeros((N_REQ * POOL * PAGE, KV_HEADS * 2 * HEAD_DIM), jnp.bfloat16).at[rows.reshape(-1)].set(key_values)
    return (layer_out, cache.reshape(N_REQ * POOL, PAGE, KV_HEADS * 2 * HEAD_DIM))
```

```python
import jax
import jax.numpy as jnp
from jax import lax
from jax.sharding import Mesh, PartitionSpec as P

HEAD_DIM = 128
PAGE = 16
SLOTS = 8
epsilon = 1e-05

AXES = ("zh", "y", "x", "c", "tp")
REQ = ("zh", "y", "x", "c")
PLANE = ("y", "x")
LINE = ("zh", "tp")
F32 = jnp.float32
BF16 = jnp.bfloat16
I32 = jnp.int32


def dot(a, b, dims):
    return lax.dot_general(a, b, (dims, ((), ())), preferred_element_type=F32)


def iota(shape, dim):
    return lax.broadcasted_iota(I32, shape, dim)


def from_ahead(value, axis, step, size):
    return lax.ppermute(value, axis, [((i + step) % size, i) for i in range(size)])


def swap_cores(value):
    return lax.ppermute(value, "c", [(0, 1), (1, 0)])


def prompt_layout(lengths, count):
    ends = [lengths[0]]
    for i in range(1, lengths.shape[0]):
        ends.append(ends[-1] + lengths[i])
    return ends


def attend(queries, key_values, segment_row, segment_col):
    count = queries.shape[0]
    heads = queries.shape[1] // HEAD_DIM
    keys, values = key_values[:, :HEAD_DIM], key_values[:, HEAD_DIM:]
    stacked = jnp.concatenate(
        [queries[:, h * HEAD_DIM : (h + 1) * HEAD_DIM] for h in range(heads)], axis=0
    )
    scores = dot(stacked, keys, ((1,), (1,))) * HEAD_DIM ** (-0.5)
    scores = scores.reshape(heads, count, count)
    allowed = (segment_col == segment_row) & (iota((count, count), 1) <= iota((count, count), 0))
    scores = jnp.where(allowed[None], scores, -1e30)
    highest = jnp.max(scores, axis=-1, keepdims=True)
    weights = jnp.exp(scores - highest)
    probs = (weights / jnp.sum(weights, axis=-1, keepdims=True)).astype(BF16)
    context = dot(probs.reshape(heads * count, count), values, ((1,), (0,))).astype(BF16)
    return jnp.concatenate(
        [context[h * count : (h + 1) * count] for h in range(heads)], axis=1
    )


def routing(choice_t, weight_t, first, own_experts, blocks):
    top, tokens = choice_t.shape
    count = tokens // blocks
    local = (choice_t - first).T
    weight = weight_t.T
    named = jnp.zeros((tokens, own_experts), F32)
    routed = jnp.zeros((tokens, own_experts), F32)
    places = iota((tokens, own_experts), 1)
    for k in range(top):
        hit = local[:, k : k + 1] == places
        named = named + hit.astype(F32)
        routed = routed + jnp.where(hit, weight[:, k : k + 1], 0.0)
    here, before = iota((tokens, tokens), 0), iota((tokens, tokens), 1)
    earlier = ((before < here) & (before // count == here // count)).astype(BF16)
    named = named.astype(BF16)
    ranks = dot(earlier, named, ((1,), (0,))).astype(BF16)
    high = lax.reduce_precision(routed, 8, 7)
    low = (routed - high).astype(BF16)
    high = high.astype(BF16)
    rows = own_experts * blocks * SLOTS
    spread = (
        iota((own_experts, rows), 1) // (blocks * SLOTS) == iota((own_experts, rows), 0)
    ).astype(BF16)
    column = iota((tokens, rows), 1)
    mine = (column // SLOTS) % blocks == iota((tokens, rows), 0) // count
    taken = (
        mine
        & (dot(named, spread, ((1,), (0,))) > 0.5)
        & (dot(ranks, spread, ((1,), (0,))).astype(I32) == column % SLOTS)
    )
    selector = taken.astype(BF16)
    parts = [
        jnp.where(taken, dot(part, spread, ((1,), (0,))), 0.0).astype(BF16)
        for part in (high, low)
    ]
    return selector, parts


def normalize(mid, gain):
    wide = mid.astype(F32)
    square = jnp.mean(wide * wide, axis=1, keepdims=True)
    return (wide * lax.rsqrt(square + epsilon) * gain).astype(BF16)


def features_joined(pieces):
    return jnp.concatenate(pieces, axis=1)


def experts_of(rows, weights):
    total = None
    for gate_up, down in weights:
        units = down.shape[0]
        projected = dot(rows, gate_up, ((1,), (0,)))
        activated = (jax.nn.silu(projected[:, :units]) * projected[:, units:]).astype(BF16)
        part = dot(activated, down, ((1,), (0,)))
        total = part if total is None else total + part
    return total.astype(BF16)


def combined(returned, parts):
    high, low = parts
    return dot(high, returned, ((1,), (0,))) + dot(low, returned, ((1,), (0,)))


def on_device(
    queries,
    key_values,
    hidden,
    lengths,
    page_table,
    out_weight,
    norm_gain,
    expert_choice,
    route_weight,
    gate_up,
    down,
):
    count = queries.shape[0]
    width = hidden.shape[1]
    n_zh, n_tp = lax.axis_size("zh"), lax.axis_size("tp")
    planes = lax.axis_size("y") * lax.axis_size("x")
    zh, tp = lax.axis_index("zh"), lax.axis_index("tp")
    share = width // n_tp
    own_start = tp * share
    columns = out_weight.shape[1]

    weight_t = out_weight.T
    shards = [
        lax.ppermute(
            weight_t,
            LINE,
            [(a * n_tp + b, ((b - k) % n_zh) * n_tp + a) for a in range(n_zh) for b in range(n_tp)],
        )
        for k in range(n_zh)
    ]
    choice_t = expert_choice.T
    rw_t = route_weight.T
    choices = [choice_t] + [from_ahead(choice_t, "zh", j, n_zh) for j in range(1, n_zh)]
    route = [rw_t] + [from_ahead(rw_t, "zh", j, n_zh) for j in range(1, n_zh)]

    row = lengths[0]
    places = jnp.arange(count, dtype=I32)
    ends = jnp.cumsum(row)
    starts = ends - row
    segment = jnp.sum((ends[None, :] <= places[:, None]).astype(I32), axis=1)
    picked = segment[:, None] == jnp.arange(row.shape[0], dtype=I32)[None, :]
    offset = places - jnp.sum(jnp.where(picked, starts[None, :], 0), axis=1)

    context = attend(queries, key_values, segment[None, :], segment[:, None])
    contexts = jnp.stack([context] + [from_ahead(context, "tp", j, n_tp) for j in range(1, n_tp)])

    sent = jnp.concatenate(shards, axis=0)
    sent = jnp.broadcast_to(sent[None], (planes,) + sent.shape)
    half = lax.all_to_all(sent, PLANE, 0, 0, tiled=True)
    other = swap_cores(half)

    gate_up_own, down_own = gate_up[0], down[0]
    weights = ((gate_up_own, down_own), (swap_cores(gate_up_own), swap_cores(down_own)))

    blocks = [
        lax.dynamic_index_in_dim(contexts, (zh + k - tp) % n_tp, 0, keepdims=False)
        for k in range(n_zh)
    ]
    stacked = jnp.concatenate(blocks, axis=0)
    halves = []
    for piece in (half, other):
        full = dot(stacked, piece.reshape(-1, piece.shape[2]), ((1,), (1,)))
        full = full.reshape(n_zh, count, planes, n_zh, columns)
        halves.append(sum(full[k, :, :, k, :] for k in range(n_zh)))
    core = lax.axis_index("c")
    first = jnp.where(core == 0, halves[0], halves[1])
    second = jnp.where(core == 0, halves[1], halves[0])
    attn = jnp.stack([first, second], axis=2).reshape(count, share)
    hidden_own = lax.dynamic_slice_in_dim(hidden, own_start, share, 1)
    mid_own = (hidden_own.astype(F32) + attn).astype(BF16)
    mid_own = lax.optimization_barrier(mid_own)

    distant = jnp.concatenate([from_ahead(mid_own, "zh", j, n_zh) for j in range(1, n_zh)], axis=0)
    near = lax.all_gather(mid_own, "tp")
    near = features_joined([near[i] for i in range(n_tp)])
    far = [distant] + [from_ahead(distant, "tp", j, n_tp) for j in range(1, n_tp)]
    far = jnp.stack(far)
    own_experts = planes
    first_expert = zh * own_experts
    near_sel, near_parts = routing(choices[0], route[0], first_expert, own_experts, 1)
    far_sel, far_parts = routing(
        jnp.concatenate(choices[1:], axis=1),
        jnp.concatenate(route[1:], axis=1),
        first_expert,
        own_experts,
        n_zh - 1,
    )
    near_rows = dot(near_sel, normalize(near, norm_gain), ((0,), (0,))).astype(BF16)
    near_rows = near_rows.reshape(planes, SLOTS, width)
    near_in = lax.all_to_all(near_rows, PLANE, 0, 0, tiled=True)
    far_mid = features_joined(
        [
            lax.dynamic_index_in_dim(far, (i - tp) % n_tp, 0, keepdims=False)
            for i in range(n_tp)
        ]
    )
    far_rows = dot(far_sel, normalize(far_mid, norm_gain), ((0,), (0,))).astype(BF16)
    far_rows = far_rows.reshape(planes, (n_zh - 1) * SLOTS, width)
    far_in = lax.all_to_all(far_rows, PLANE, 0, 0, tiled=True)

    far_out = experts_of(far_in.reshape(-1, width), weights).reshape(far_in.shape)
    far_back = lax.all_to_all(far_out, PLANE, 0, 0, tiled=True)
    near_out = experts_of(near_in.reshape(-1, width), weights).reshape(near_in.shape)
    near_back = lax.all_to_all(near_out, PLANE, 0, 0, tiled=True)

    far_moe = combined(far_back.reshape(-1, width), far_parts).astype(BF16)
    far_quarters = jnp.stack([far_moe[:, i * share : (i + 1) * share] for i in range(n_tp)])
    far_sum = lax.dynamic_index_in_dim(far_quarters, tp, 0, keepdims=False).astype(F32)
    for j in range(1, n_tp):
        piece = lax.dynamic_index_in_dim(far_quarters, (tp - j) % n_tp, 0, keepdims=False)
        far_sum = far_sum + from_ahead(piece, "tp", j, n_tp).astype(F32)
    far_sum = far_sum.astype(BF16)
    near_moe = combined(near_back.reshape(-1, width), near_parts).astype(BF16)
    near_quarters = jnp.stack([near_moe[:, i * share : (i + 1) * share] for i in range(n_tp)])
    near_got = lax.all_to_all(near_quarters, "tp", 0, 0, tiled=True)
    moe = jnp.sum(near_got.astype(F32), axis=0)
    for j in range(1, n_zh):
        moe = moe + from_ahead(far_sum[(j - 1) * count : j * count], "zh", -j, n_zh).astype(F32)
    layer_out = (mid_own.astype(F32) + moe).astype(BF16)

    pages = page_table[0]
    flat_pages = pages.reshape(-1)
    pool = flat_pages.shape[0]
    page_of = segment * pages.shape[1] + offset // PAGE
    slot_page = jnp.sum(
        jnp.where(
            page_of[:, None] == jnp.arange(pool, dtype=I32)[None, :], flat_pages[None, :], 0
        ),
        axis=1,
    )
    cache_rows = slot_page * PAGE + offset % PAGE
    put = (iota((pool * PAGE, count), 0) == cache_rows[None, :]).astype(BF16)
    cache = dot(put, key_values, ((1,), (0,))).astype(BF16)
    return (layer_out, cache.reshape(pool, PAGE, key_values.shape[1]))


def solution(mesh):
    grid = Mesh(mesh.devices.reshape(4, 4, 4, 2, 4), AXES)
    placed = (
        P(REQ, "tp"),
        P(REQ, "tp"),
        P(REQ, None),
        P(REQ, None),
        P(REQ, None, None),
        P("tp", REQ),
        P(),
        P(REQ, None),
        P(REQ, None),
        P(REQ, None, "tp"),
        P(REQ, "tp", None),
    )
    return jax.shard_map(
        on_device,
        mesh=grid,
        in_specs=placed,
        out_specs=(P(REQ, "tp"), P(REQ, None, "tp")),
        check_vma=False,
    )
```

```python
import jax
import jax.numpy as jnp
from jax import lax
from jax.sharding import Mesh, PartitionSpec as P

HEAD_DIM = 128
PAGE = 16
SLOTS = 8
epsilon = 1e-05

AXES = ("zh", "y", "x", "c", "tp")
REQ = ("zh", "y", "x", "c")
PLANE = ("y", "x")
LINE = ("zh", "tp")
F32 = jnp.float32
BF16 = jnp.bfloat16
I32 = jnp.int32


def dot(a, b, dims):
    return lax.dot_general(a, b, (dims, ((), ())), preferred_element_type=F32)


def iota(shape, dim):
    return lax.broadcasted_iota(I32, shape, dim)


def swapped(value, axis, size, mate):
    return lax.ppermute(value, axis, [(i, mate(i)) for i in range(size)])


def swap_cores(value):
    return swapped(value, "c", 2, lambda i: 1 - i)


def swap_units(value):
    return swapped(value, "tp", 4, lambda i: i ^ 1)


def swap_groups(value):
    return swapped(value, "tp", 4, lambda i: 3 - i)


def turned(value):
    return swapped(value, LINE, 16, lambda i: i % 4 * 4 + i // 4)


def spread_to_all(value, axis, size):
    copies = jnp.broadcast_to(value[None], (size,) + value.shape)
    return lax.all_to_all(copies, axis, 0, 0, tiled=True)


def attend(queries, key_values, segment_row, segment_col):
    count = queries.shape[0]
    heads = queries.shape[1] // HEAD_DIM
    keys, values = key_values[:, :HEAD_DIM], key_values[:, HEAD_DIM:]
    stacked = jnp.concatenate(
        [queries[:, h * HEAD_DIM : (h + 1) * HEAD_DIM] for h in range(heads)], axis=0
    )
    scores = dot(stacked, keys, ((1,), (1,))) * HEAD_DIM ** (-0.5)
    scores = scores.reshape(heads, count, count)
    allowed = (segment_col == segment_row) & (iota((count, count), 1) <= iota((count, count), 0))
    scores = jnp.where(allowed[None], scores, -1e30)
    highest = jnp.max(scores, axis=-1, keepdims=True)
    weights = jnp.exp(scores - highest)
    probs = (weights / jnp.sum(weights, axis=-1, keepdims=True)).astype(BF16)
    context = dot(probs.reshape(heads * count, count), values, ((1,), (0,))).astype(BF16)
    return jnp.concatenate(
        [context[h * count : (h + 1) * count] for h in range(heads)], axis=1
    )


def packed_routing(choice, weight):
    high = lax.reduce_precision(weight, 8, 7)
    packed = jnp.concatenate([choice.astype(F32), high, weight - high], axis=1)
    return jnp.pad(packed, ((0, 0), (0, 128 - packed.shape[1]))).astype(BF16)


def routing(packed, top, first, own_experts):
    tokens = packed.shape[0]
    local = packed[:, :top].astype(F32) - first.astype(F32)
    high, low = (packed[:, top * i : top * (i + 1)].astype(F32) for i in (1, 2))
    rows = own_experts * SLOTS
    expert = (iota((tokens, rows), 1) // SLOTS).astype(F32)
    slot = (iota((tokens, rows), 1) % SLOTS).astype(F32)
    named = jnp.zeros((tokens, rows), F32)
    highs = jnp.zeros((tokens, rows), F32)
    lows = jnp.zeros((tokens, rows), F32)
    for k in range(top):
        hit = local[:, k : k + 1] == expert
        named = jnp.where(hit, 1.0, named)
        highs = jnp.where(hit, high[:, k : k + 1], highs)
        lows = jnp.where(hit, low[:, k : k + 1], lows)
    earlier = (iota((tokens, tokens), 1) < iota((tokens, tokens), 0)).astype(BF16)
    ranks = dot(earlier, named.astype(BF16), ((1,), (0,)))
    taken = (named > 0.5) & (ranks == slot)
    parts = [jnp.where(taken, part, 0.0).astype(BF16) for part in (highs, lows)]
    return taken.astype(BF16), parts


def normalize(mid, gain):
    wide = mid.astype(F32)
    square = jnp.mean(wide * wide, axis=1, keepdims=True)
    return (wide * lax.rsqrt(square + epsilon) * gain).astype(BF16)


def experts_of(rows, weights):
    total = None
    for gate_up, down in weights:
        units = down.shape[0]
        projected = dot(rows, gate_up, ((1,), (0,)))
        activated = (jax.nn.silu(projected[:, :units]) * projected[:, units:]).astype(BF16)
        part = dot(activated, down, ((1,), (0,)))
        total = part if total is None else total + part
    return total.astype(BF16)


def combined(returned, parts):
    high, low = parts
    return dot(high, returned, ((1,), (0,))) + dot(low, returned, ((1,), (0,)))


def on_device(
    queries,
    key_values,
    hidden,
    lengths,
    page_table,
    out_weight,
    norm_gain,
    expert_choice,
    route_weight,
    gate_up,
    down,
):
    count = queries.shape[0]
    width = hidden.shape[1]
    n_zh, n_tp = lax.axis_size("zh"), lax.axis_size("tp")
    planes = lax.axis_size("y") * lax.axis_size("x")
    zh, tp = lax.axis_index("zh"), lax.axis_index("tp")
    share = width // n_tp
    top = expert_choice.shape[1]
    gate_up_own, down_own = gate_up[0], down[0]

    projection = spread_to_all(out_weight.T, ("y", "x", "c"), 2 * planes)
    projection = projection.reshape(share, out_weight.shape[0])

    row = lengths[0]
    places = jnp.arange(count, dtype=I32)
    ends = jnp.cumsum(row)
    starts = ends - row
    segment = jnp.sum((ends[None, :] <= places[:, None]).astype(I32), axis=1)
    picked = segment[:, None] == jnp.arange(row.shape[0], dtype=I32)[None, :]
    offset = places - jnp.sum(jnp.where(picked, starts[None, :], 0), axis=1)

    context = attend(queries, key_values, segment[None, :], segment[:, None])
    contexts = spread_to_all(context, "zh", n_zh)

    hidden_own = turned(lax.dynamic_slice_in_dim(hidden, tp * share, share, 1))
    near_packed = turned(packed_routing(expert_choice, route_weight))
    far_packed = swap_groups(near_packed)

    weights = [(gate_up_own, down_own)]
    weights.append((swap_units(gate_up_own), swap_units(down_own)))
    weights.append((swap_cores(gate_up_own), swap_cores(down_own)))
    weights.append((swap_cores(weights[1][0]), swap_cores(weights[1][1])))

    partial = dot(contexts.reshape(n_zh * count, -1), projection, ((1,), (1,))).astype(BF16)
    partial = lax.all_to_all(
        partial.reshape(n_zh, count, share), "tp", 0, 0, tiled=True
    )
    attn = jnp.sum(partial.astype(F32), axis=0)
    mid_own = (hidden_own.astype(F32) + attn).astype(BF16)
    mid_own = lax.optimization_barrier(mid_own)

    blocks = spread_to_all(mid_own, "zh", n_zh)
    near = jnp.concatenate([blocks[i] for i in range(n_zh)], axis=1)
    far = swap_groups(near)
    first = zh * planes

    def sent(mid, packed):
        selector, parts = routing(packed, top, first, planes)
        rows = dot(selector, normalize(mid, norm_gain), ((0,), (0,))).astype(BF16)
        rows = rows.reshape(planes, SLOTS, width)
        return lax.all_to_all(rows, PLANE, 0, 0, tiled=True), parts

    near_in, near_parts = sent(near, near_packed)
    far_in, far_parts = sent(far, far_packed)
    near_out = experts_of(near_in.reshape(-1, width), weights).reshape(near_in.shape)
    far_out = experts_of(far_in.reshape(-1, width), weights).reshape(far_in.shape)
    far_back = lax.all_to_all(far_out, PLANE, 0, 0, tiled=True)
    far_back, near_out = lax.optimization_barrier((far_back, near_out))
    near_back = lax.all_to_all(near_out, PLANE, 0, 0, tiled=True)

    far_moe = combined(far_back.reshape(-1, width), far_parts).astype(BF16)
    near_moe = combined(near_back.reshape(-1, width), near_parts)
    near_moe = (near_moe + swap_groups(far_moe).astype(F32)).astype(BF16)
    columns = jnp.stack([near_moe[:, i * share : (i + 1) * share] for i in range(n_zh)])
    gathered = lax.all_to_all(columns, "zh", 0, 0, tiled=True)
    moe = jnp.sum(gathered.astype(F32), axis=0)
    layer_out = turned((mid_own.astype(F32) + moe).astype(BF16))

    pages = page_table[0]
    flat_pages = pages.reshape(-1)
    pool = flat_pages.shape[0]
    page_of = segment * pages.shape[1] + offset // PAGE
    slot_page = jnp.sum(
        jnp.where(
            page_of[:, None] == jnp.arange(pool, dtype=I32)[None, :], flat_pages[None, :], 0
        ),
        axis=1,
    )
    cache_rows = slot_page * PAGE + offset % PAGE
    put = (iota((pool * PAGE, count), 0) == cache_rows[None, :]).astype(BF16)
    cache = dot(put, key_values, ((1,), (0,))).astype(BF16)
    return (layer_out, cache.reshape(pool, PAGE, key_values.shape[1]))


def solution(mesh):
    grid = Mesh(mesh.devices.reshape(4, 4, 4, 2, 4), AXES)
    placed = (
        P(REQ, "tp"),
        P(REQ, "tp"),
        P(REQ, None),
        P(REQ, None),
        P(REQ, None, None),
        P("tp", REQ),
        P(),
        P(REQ, None),
        P(REQ, None),
        P(REQ, None, "tp"),
        P(REQ, "tp", None),
    )
    return jax.shard_map(
        on_device,
        mesh=grid,
        in_specs=placed,
        out_specs=(P(REQ, "tp"), P(REQ, None, "tp")),
        check_vma=False,
    )
```

```python
import functools

import jax
import jax.numpy as jnp
from jax import lax
from jax.experimental import pallas as pl
from jax.experimental.pallas import tpu as pltpu
from jax.sharding import Mesh, PartitionSpec as P


HEAD_DIM = 128
PAGE = 16
SLOTS = 8
epsilon = 1e-05

AXES = ("zh", "y", "x", "c", "tp")
REQ = ("zh", "y", "x", "c")
PLANE = ("y", "x")
LINE = ("zh", "tp")
F32 = jnp.float32
BF16 = jnp.bfloat16
I32 = jnp.int32


def dot(a, b, dims):
    return lax.dot_general(a, b, (dims, ((), ())), preferred_element_type=F32)


def iota(shape, dim):
    return lax.broadcasted_iota(I32, shape, dim)


def from_ahead(value, axis, step, size):
    return lax.ppermute(value, axis, [((i + step) % size, i) for i in range(size)])


def swapped(value, axis, size, mate):
    return lax.ppermute(value, axis, [(i, mate(i)) for i in range(size)])


def swap_cores(value):
    return swapped(value, "c", 2, lambda i: 1 - i)


def swap_units(value):
    return swapped(value, "tp", 4, lambda i: i ^ 1)


def swap_groups(value):
    return swapped(value, "tp", 4, lambda i: 3 - i)


def turned(value):
    return swapped(value, LINE, 16, lambda i: i % 4 * 4 + i // 4)


def spread_to_all(value, axis, size):
    copies = jnp.broadcast_to(value[None], (size,) + value.shape)
    return lax.all_to_all(copies, axis, 0, 0, tiled=True)


def attend(queries, key_values, segment_row, segment_col):
    count = queries.shape[0]
    heads = queries.shape[1] // HEAD_DIM
    keys, values = key_values[:, :HEAD_DIM], key_values[:, HEAD_DIM:]
    stacked = jnp.concatenate(
        [queries[:, h * HEAD_DIM : (h + 1) * HEAD_DIM] for h in range(heads)], axis=0
    )
    scores = dot(stacked, keys, ((1,), (1,))) * HEAD_DIM ** (-0.5)
    scores = scores.reshape(heads, count, count)
    allowed = (segment_col == segment_row) & (iota((count, count), 1) <= iota((count, count), 0))
    scores = jnp.where(allowed[None], scores, -1e30)
    highest = jnp.max(scores, axis=-1, keepdims=True)
    weights = jnp.exp(scores - highest)
    probs = (weights / jnp.sum(weights, axis=-1, keepdims=True)).astype(BF16)
    context = dot(probs.reshape(heads * count, count), values, ((1,), (0,))).astype(BF16)
    return jnp.concatenate(
        [context[h * count : (h + 1) * count] for h in range(heads)], axis=1
    )


def packed_routing(choice, weight):
    high = lax.reduce_precision(weight, 8, 7)
    packed = jnp.concatenate([choice.astype(F32), high, weight - high], axis=1)
    return jnp.pad(packed, ((0, 0), (0, 128 - packed.shape[1]))).astype(BF16)


def routing(packed, top, first, own_experts):
    tokens = packed.shape[0]
    local = packed[:, :top].astype(F32) - first.astype(F32)
    high, low = (packed[:, top * i : top * (i + 1)].astype(F32) for i in (1, 2))
    rows = own_experts * SLOTS
    expert = (iota((tokens, rows), 1) // SLOTS).astype(F32)
    slot = (iota((tokens, rows), 1) % SLOTS).astype(F32)
    named = jnp.zeros((tokens, rows), F32)
    highs = jnp.zeros((tokens, rows), F32)
    lows = jnp.zeros((tokens, rows), F32)
    for k in range(top):
        hit = local[:, k : k + 1] == expert
        named = jnp.where(hit, 1.0, named)
        highs = jnp.where(hit, high[:, k : k + 1], highs)
        lows = jnp.where(hit, low[:, k : k + 1], lows)
    earlier = (iota((tokens, tokens), 1) < iota((tokens, tokens), 0)).astype(BF16)
    ranks = dot(earlier, named.astype(BF16), ((1,), (0,)))
    taken = (named > 0.5) & (ranks == slot)
    parts = [jnp.where(taken, part, 0.0).astype(BF16) for part in (highs, lows)]
    return taken.astype(BF16), parts


def normalize(mid, gain):
    wide = mid.astype(F32)
    square = jnp.mean(wide * wide, axis=1, keepdims=True)
    return (wide * lax.rsqrt(square + epsilon) * gain).astype(BF16)


def experts_kernel(groups, rows_ref, *refs):
    sources, (out_ref, gate_up, down, total, arrived) = refs[: 2 * groups], refs[2 * groups :]
    copies = []
    for group in range(groups):
        for i, target in enumerate((gate_up, down)):
            number = 2 * group + i
            copies.append(
                pltpu.make_async_copy(sources[number], target.at[group], arrived.at[number])
            )
    for copy in copies:
        copy.start()
    units = down.shape[1]
    for group in range(groups):
        copies[2 * group].wait()
        projected = jnp.dot(rows_ref[...], gate_up[group], preferred_element_type=F32)
        gate, upper = projected[:, :units], projected[:, units:]
        activated = (gate / (1.0 + jnp.exp(-gate)) * upper).astype(BF16)
        copies[2 * group + 1].wait()
        part = jnp.dot(activated, down[group], preferred_element_type=F32)
        if group == 0:
            total[...] = part
        else:
            total[...] += part
    out_ref[...] = total[...].astype(BF16)


def experts_of(rows, gate_ups, downs):
    groups = len(gate_ups)
    operands = [a for both in zip(gate_ups, downs) for a in both]
    vmem = pl.BlockSpec(memory_space=pltpu.VMEM)
    anywhere = pl.BlockSpec(memory_space=pl.ANY)
    return pl.pallas_call(
        functools.partial(experts_kernel, groups),
        out_shape=jax.ShapeDtypeStruct(rows.shape, BF16),
        in_specs=[vmem] + [anywhere] * len(operands),
        out_specs=vmem,
        scratch_shapes=[
            pltpu.VMEM((groups,) + gate_ups[0].shape, BF16),
            pltpu.VMEM((groups,) + downs[0].shape, BF16),
            pltpu.VMEM(rows.shape, F32),
            pltpu.SemaphoreType.DMA((len(operands),)),
        ],
        name="experts",
    )(rows, *operands)


def combined(returned, parts):
    high, low = parts
    return dot(high, returned, ((1,), (0,))) + dot(low, returned, ((1,), (0,)))


def layer(
    queries,
    key_values,
    hidden,
    lengths,
    page_table,
    out_weight,
    norm_gain,
    expert_choice,
    route_weight,
    gate_up,
    down,
):
    count = queries.shape[0]
    width = hidden.shape[1]
    n_zh, n_tp = lax.axis_size("zh"), lax.axis_size("tp")
    planes = lax.axis_size("y") * lax.axis_size("x")
    zh, tp = lax.axis_index("zh"), lax.axis_index("tp")
    share = width // n_tp
    top = expert_choice.shape[1]
    gate_up_own, down_own = gate_up[0], down[0]

    pair_gate_up = swap_units(gate_up_own)
    pair_down = swap_units(down_own)

    projection = spread_to_all(out_weight.T, ("y", "x", "c"), 2 * planes)
    projection = projection.reshape(share, out_weight.shape[0])

    row = lengths[0]
    places = jnp.arange(count, dtype=I32)
    ends = jnp.cumsum(row)
    starts = ends - row
    segment = jnp.sum((ends[None, :] <= places[:, None]).astype(I32), axis=1)
    picked = segment[:, None] == jnp.arange(row.shape[0], dtype=I32)[None, :]
    offset = places - jnp.sum(jnp.where(picked, starts[None, :], 0), axis=1)

    context = attend(queries, key_values, segment[None, :], segment[:, None])
    contexts = [context]
    for j in range(1, n_zh):
        contexts.append(from_ahead(context, "zh", j, n_zh))
    contexts = jnp.stack(contexts)
    contexts = jnp.concatenate(
        [
            lax.dynamic_index_in_dim(contexts, (i - zh) % n_zh, 0, keepdims=False)
            for i in range(n_zh)
        ],
        axis=0,
    )

    hidden_own = turned(lax.dynamic_slice_in_dim(hidden, tp * share, share, 1))
    near_packed = packed_routing(expert_choice, route_weight)
    near_packed = turned(near_packed)
    far_packed = swap_groups(near_packed)

    gate_ups = [gate_up_own, swap_cores(gate_up_own), pair_gate_up, swap_cores(pair_gate_up)]
    downs = [down_own, swap_cores(down_own), pair_down, swap_cores(pair_down)]

    partial = dot(contexts, projection, ((1,), (1,))).astype(BF16)
    partial = lax.all_to_all(
        partial.reshape(n_zh, count, share), "tp", 0, 0, tiled=True
    )
    attn = jnp.sum(partial.astype(F32), axis=0)
    mid_own = (hidden_own.astype(F32) + attn).astype(BF16)
    mid_own = lax.optimization_barrier(mid_own)

    blocks = spread_to_all(mid_own, "zh", n_zh)
    near = jnp.concatenate([blocks[i] for i in range(n_zh)], axis=1)
    far = swap_groups(near)
    first = zh * planes

    def sent(mid, packed):
        selector, parts = routing(packed, top, first, planes)
        rows = dot(selector, normalize(mid, norm_gain), ((0,), (0,))).astype(BF16)
        rows = rows.reshape(planes, SLOTS, width)
        return lax.all_to_all(rows, PLANE, 0, 0, tiled=True), parts

    near_in, near_parts = sent(near, near_packed)
    far_in, far_parts = sent(far, far_packed)
    near_out = experts_of(near_in.reshape(-1, width), gate_ups, downs).reshape(near_in.shape)
    far_out = experts_of(far_in.reshape(-1, width), gate_ups, downs).reshape(far_in.shape)
    far_back = lax.all_to_all(far_out, PLANE, 0, 0, tiled=True)
    far_back, near_out = lax.optimization_barrier((far_back, near_out))
    near_back = lax.all_to_all(near_out, PLANE, 0, 0, tiled=True)

    far_moe = combined(far_back.reshape(-1, width), far_parts).astype(BF16)
    near_moe = combined(near_back.reshape(-1, width), near_parts)
    near_moe = (near_moe + swap_groups(far_moe).astype(F32)).astype(BF16)
    columns = jnp.stack([near_moe[:, i * share : (i + 1) * share] for i in range(n_zh)])
    gathered = lax.all_to_all(columns, "zh", 0, 0, tiled=True)
    moe = jnp.sum(gathered.astype(F32), axis=0)
    layer_out = turned((mid_own.astype(F32) + moe).astype(BF16))

    pages = page_table[0]
    flat_pages = pages.reshape(-1)
    pool = flat_pages.shape[0]
    page_of = segment * pages.shape[1] + offset // PAGE
    slot_page = jnp.sum(
        jnp.where(
            page_of[:, None] == jnp.arange(pool, dtype=I32)[None, :], flat_pages[None, :], 0
        ),
        axis=1,
    )
    cache_rows = slot_page * PAGE + offset % PAGE
    put = (iota((pool * PAGE, count), 0) == cache_rows[None, :]).astype(BF16)
    cache = dot(put, key_values, ((1,), (0,))).astype(BF16)
    return (layer_out, cache.reshape(pool, PAGE, key_values.shape[1]))


def solution(mesh):
    grid = Mesh(mesh.devices.reshape(4, 4, 4, 2, 4), AXES)
    placed = (
        P(REQ, "tp"),
        P(REQ, "tp"),
        P(REQ, None),
        P(REQ, None),
        P(REQ, None, None),
        P("tp", REQ),
        P(),
        P(REQ, None),
        P(REQ, None),
        P(REQ, None, "tp"),
        P(REQ, "tp", None),
    )
    return jax.shard_map(
        layer,
        mesh=grid,
        in_specs=placed,
        out_specs=(P(REQ, "tp"), P(REQ, None, "tp")),
        check_vma=False,
    )
```

```python
import functools

import jax
import jax.numpy as jnp
from jax import lax
from jax.experimental import pallas as pl
from jax.experimental.pallas import tpu as pltpu
from jax.sharding import Mesh, PartitionSpec as P


HEAD_DIM = 128
PAGE = 16
SLOTS = 8
epsilon = 1e-05

AXES = ("zh", "y", "x", "c", "tp")
REQ = ("zh", "y", "x", "c")
PLANE = ("y", "x")
LINE = ("zh", "tp")
F32 = jnp.float32
BF16 = jnp.bfloat16
I32 = jnp.int32


def dot(a, b, dims):
    return lax.dot_general(a, b, (dims, ((), ())), preferred_element_type=F32)


def iota(shape, dim):
    return lax.broadcasted_iota(I32, shape, dim)


def from_ahead(value, axis, step, size):
    return lax.ppermute(value, axis, [((i + step) % size, i) for i in range(size)])


def swapped(value, axis, size, mate):
    return lax.ppermute(value, axis, [(i, mate(i)) for i in range(size)])


def swap_cores(value):
    return swapped(value, "c", 2, lambda i: 1 - i)


def swap_units(value):
    return swapped(value, "tp", 4, lambda i: i ^ 1)


def swap_groups(value):
    return swapped(value, "tp", 4, lambda i: 3 - i)


def turned(value):
    return swapped(value, LINE, 16, lambda i: i % 4 * 4 + i // 4)


def spread_to_all(value, axis, size):
    copies = jnp.broadcast_to(value[None], (size,) + value.shape)
    return lax.all_to_all(copies, axis, 0, 0, tiled=True)


def attend(queries, key_values, segment_row, segment_col):
    count = queries.shape[0]
    heads = queries.shape[1] // HEAD_DIM
    keys, values = key_values[:, :HEAD_DIM], key_values[:, HEAD_DIM:]
    stacked = jnp.concatenate(
        [queries[:, h * HEAD_DIM : (h + 1) * HEAD_DIM] for h in range(heads)], axis=0
    )
    scores = dot(stacked, keys, ((1,), (1,))) * HEAD_DIM ** (-0.5)
    scores = scores.reshape(heads, count, count)
    allowed = (segment_col == segment_row) & (iota((count, count), 1) <= iota((count, count), 0))
    scores = jnp.where(allowed[None], scores, -1e30)
    highest = jnp.max(scores, axis=-1, keepdims=True)
    weights = jnp.exp(scores - highest)
    probs = (weights / jnp.sum(weights, axis=-1, keepdims=True)).astype(BF16)
    context = dot(probs.reshape(heads * count, count), values, ((1,), (0,))).astype(BF16)
    return jnp.concatenate(
        [context[h * count : (h + 1) * count] for h in range(heads)], axis=1
    )


def packed_routing(choice, weight):
    high = lax.reduce_precision(weight, 8, 7)
    packed = jnp.concatenate([choice.astype(F32), high, weight - high], axis=1)
    return jnp.pad(packed, ((0, 0), (0, 128 - packed.shape[1]))).astype(BF16)


def routing(packed, top, first, own_experts):
    tokens = packed.shape[0]
    local = packed[:, :top].astype(F32) - first.astype(F32)
    high, low = (packed[:, top * i : top * (i + 1)].astype(F32) for i in (1, 2))
    rows = own_experts * SLOTS
    expert = (iota((tokens, rows), 1) // SLOTS).astype(F32)
    slot = (iota((tokens, rows), 1) % SLOTS).astype(F32)
    named = jnp.zeros((tokens, rows), F32)
    highs = jnp.zeros((tokens, rows), F32)
    lows = jnp.zeros((tokens, rows), F32)
    for k in range(top):
        hit = local[:, k : k + 1] == expert
        named = jnp.where(hit, 1.0, named)
        highs = jnp.where(hit, high[:, k : k + 1], highs)
        lows = jnp.where(hit, low[:, k : k + 1], lows)
    earlier = (iota((tokens, tokens), 1) < iota((tokens, tokens), 0)).astype(BF16)
    ranks = dot(earlier, named.astype(BF16), ((1,), (0,)))
    taken = (named > 0.5) & (ranks == slot)
    parts = [jnp.where(taken, part, 0.0).astype(BF16) for part in (highs, lows)]
    return taken.astype(BF16), parts


def normalize(mid, gain):
    wide = mid.astype(F32)
    square = jnp.mean(wide * wide, axis=1, keepdims=True)
    return (wide * lax.rsqrt(square + epsilon) * gain).astype(BF16)


def experts_kernel(layout, rows_ref, *refs):
    count = sum(len(part) for parts in layout for part in parts)
    sources, (out_ref, gate_up, down, total, arrived) = refs[:count], refs[count:]
    copies = []
    for group, (up_parts, down_parts) in enumerate(layout):
        own = []
        for target, parts in ((gate_up, up_parts), (down, down_parts)):
            start = 0
            for size in parts:
                i = len(copies) + len(own)
                own.append(
                    pltpu.make_async_copy(
                        sources[i], target.at[group, pl.ds(start, size)], arrived.at[i]
                    )
                )
                start += size
        copies += own
    for copy in copies:
        copy.start()
    units = down.shape[1]
    position = 0
    for group, (up_parts, down_parts) in enumerate(layout):
        for _ in up_parts:
            copies[position].wait()
            position += 1
        projected = jnp.dot(rows_ref[...], gate_up[group], preferred_element_type=F32)
        gate, upper = projected[:, :units], projected[:, units:]
        activated = (gate / (1.0 + jnp.exp(-gate)) * upper).astype(BF16)
        for _ in down_parts:
            copies[position].wait()
            position += 1
        part = jnp.dot(activated, down[group], preferred_element_type=F32)
        if group == 0:
            total[...] = part
        else:
            total[...] += part
    out_ref[...] = total[...].astype(BF16)


def experts_of(rows, gate_ups, downs):
    layout = tuple(
        (tuple(a.shape[0] for a in ups), tuple(a.shape[0] for a in lows))
        for ups, lows in zip(gate_ups, downs)
    )
    operands = [a for ups, lows in zip(gate_ups, downs) for a in (*ups, *lows)]
    groups, (depth, columns), units = len(gate_ups), gate_ups[0][0].shape, downs[0][0].shape[0]
    vmem = pl.BlockSpec(memory_space=pltpu.VMEM)
    anywhere = pl.BlockSpec(memory_space=pl.ANY)
    return pl.pallas_call(
        functools.partial(experts_kernel, layout),
        out_shape=jax.ShapeDtypeStruct(rows.shape, BF16),
        in_specs=[vmem] + [anywhere] * len(operands),
        out_specs=vmem,
        scratch_shapes=[
            pltpu.VMEM((groups, depth, columns), BF16),
            pltpu.VMEM((groups, units, depth), BF16),
            pltpu.VMEM(rows.shape, F32),
            pltpu.SemaphoreType.DMA((len(operands),)),
        ],
        name="experts",
    )(rows, *operands)


def combined(returned, parts):
    high, low = parts
    return dot(high, returned, ((1,), (0,))) + dot(low, returned, ((1,), (0,)))


def layer(
    queries,
    key_values,
    hidden,
    lengths,
    page_table,
    out_weight,
    norm_gain,
    expert_choice,
    route_weight,
    gate_up,
    down,
):
    count = queries.shape[0]
    width = hidden.shape[1]
    n_zh, n_tp = lax.axis_size("zh"), lax.axis_size("tp")
    planes = lax.axis_size("y") * lax.axis_size("x")
    zh, tp = lax.axis_index("zh"), lax.axis_index("tp")
    share = width // n_tp
    top = expert_choice.shape[1]
    gate_up_own, down_own = gate_up[0], down[0]

    cuts = (0, 2 * share, 3 * share, 4 * share)
    slices = [gate_up_own[a:b] for a, b in zip(cuts, cuts[1:])] + [down_own]
    pair = [swap_units(value) for value in slices]

    projection = spread_to_all(out_weight.T, ("y", "x", "c"), 2 * planes)
    projection = projection.reshape(share, out_weight.shape[0])

    row = lengths[0]
    places = jnp.arange(count, dtype=I32)
    ends = jnp.cumsum(row)
    starts = ends - row
    segment = jnp.sum((ends[None, :] <= places[:, None]).astype(I32), axis=1)
    picked = segment[:, None] == jnp.arange(row.shape[0], dtype=I32)[None, :]
    offset = places - jnp.sum(jnp.where(picked, starts[None, :], 0), axis=1)

    context = attend(queries, key_values, segment[None, :], segment[:, None])
    contexts = [context]
    for j in range(1, n_zh):
        contexts.append(from_ahead(context, "zh", j, n_zh))
    contexts = jnp.stack(contexts)
    contexts = jnp.concatenate(
        [
            lax.dynamic_index_in_dim(contexts, (i - zh) % n_zh, 0, keepdims=False)
            for i in range(n_zh)
        ],
        axis=0,
    )

    hidden_own = turned(lax.dynamic_slice_in_dim(hidden, tp * share, share, 1))
    near_packed = packed_routing(expert_choice, route_weight)
    near_packed = turned(near_packed)
    far_packed = swap_groups(near_packed)

    cross = [swap_cores(value) for value in pair]
    core_gate_up = swap_cores(gate_up_own)
    core_down = swap_cores(down_own)
    gate_ups = [[gate_up_own], [core_gate_up], pair[:3], cross[:3]]
    downs = [[down_own], [core_down], pair[3:], cross[3:]]

    partial = dot(contexts, projection, ((1,), (1,))).astype(BF16)
    partial = lax.all_to_all(
        partial.reshape(n_zh, count, share), "tp", 0, 0, tiled=True
    )
    attn = jnp.sum(partial.astype(F32), axis=0)
    mid_own = (hidden_own.astype(F32) + attn).astype(BF16)
    mid_own = lax.optimization_barrier(mid_own)

    blocks = spread_to_all(mid_own, "zh", n_zh)
    near = jnp.concatenate([blocks[i] for i in range(n_zh)], axis=1)
    far = swap_groups(near)
    first = zh * planes

    def sent(mid, packed):
        selector, parts = routing(packed, top, first, planes)
        rows = dot(selector, normalize(mid, norm_gain), ((0,), (0,))).astype(BF16)
        rows = rows.reshape(planes, SLOTS, width)
        return lax.all_to_all(rows, PLANE, 0, 0, tiled=True), parts

    near_in, near_parts = sent(near, near_packed)
    far_in, far_parts = sent(far, far_packed)
    near_out = experts_of(near_in.reshape(-1, width), gate_ups, downs).reshape(near_in.shape)
    far_out = experts_of(far_in.reshape(-1, width), gate_ups, downs).reshape(far_in.shape)
    far_back = lax.all_to_all(far_out, PLANE, 0, 0, tiled=True)
    far_back, near_out = lax.optimization_barrier((far_back, near_out))
    near_back = lax.all_to_all(near_out, PLANE, 0, 0, tiled=True)

    far_moe = combined(far_back.reshape(-1, width), far_parts).astype(BF16)
    near_moe = combined(near_back.reshape(-1, width), near_parts)
    near_moe = (near_moe + swap_groups(far_moe).astype(F32)).astype(BF16)
    columns = jnp.stack([near_moe[:, i * share : (i + 1) * share] for i in range(n_zh)])
    gathered = lax.all_to_all(columns, "zh", 0, 0, tiled=True)
    moe = jnp.sum(gathered.astype(F32), axis=0)
    layer_out = turned((mid_own.astype(F32) + moe).astype(BF16))

    pages = page_table[0]
    flat_pages = pages.reshape(-1)
    pool = flat_pages.shape[0]
    page_of = segment * pages.shape[1] + offset // PAGE
    slot_page = jnp.sum(
        jnp.where(
            page_of[:, None] == jnp.arange(pool, dtype=I32)[None, :], flat_pages[None, :], 0
        ),
        axis=1,
    )
    cache_rows = slot_page * PAGE + offset % PAGE
    put = (iota((pool * PAGE, count), 0) == cache_rows[None, :]).astype(BF16)
    cache = dot(put, key_values, ((1,), (0,))).astype(BF16)
    return (layer_out, cache.reshape(pool, PAGE, key_values.shape[1]))


def solution(mesh):
    grid = Mesh(mesh.devices.reshape(4, 4, 4, 2, 4), AXES)
    placed = (
        P(REQ, "tp"),
        P(REQ, "tp"),
        P(REQ, None),
        P(REQ, None),
        P(REQ, None, None),
        P("tp", REQ),
        P(),
        P(REQ, None),
        P(REQ, None),
        P(REQ, None, "tp"),
        P(REQ, "tp", None),
    )
    return jax.shard_map(
        layer,
        mesh=grid,
        in_specs=placed,
        out_specs=(P(REQ, "tp"), P(REQ, None, "tp")),
        check_vma=False,
    )
```

```python
import functools

import jax
import jax.numpy as jnp
from jax import lax
from jax.experimental import pallas as pl
from jax.experimental.pallas import tpu as pltpu
from jax.sharding import Mesh, PartitionSpec as P


HEAD_DIM = 128
PAGE = 16
SLOTS = 8
epsilon = 1e-05

AXES = ("zh", "y", "x", "c", "tp")
REQ = ("zh", "y", "x", "c")
PLANE = ("y", "x")
LINE = ("zh", "tp")
F32 = jnp.float32
BF16 = jnp.bfloat16
I32 = jnp.int32


def dot(a, b, dims):
    return lax.dot_general(a, b, (dims, ((), ())), preferred_element_type=F32)


def iota(shape, dim):
    return lax.broadcasted_iota(I32, shape, dim)


def from_ahead(value, axis, step, size):
    return lax.ppermute(value, axis, [((i + step) % size, i) for i in range(size)])


def swapped(value, axis, size, mate):
    return lax.ppermute(value, axis, [(i, mate(i)) for i in range(size)])


def swap_cores(value):
    return swapped(value, "c", 2, lambda i: 1 - i)


def swap_units(value):
    return swapped(value, "tp", 4, lambda i: i ^ 1)


def swap_groups(value):
    return swapped(value, "tp", 4, lambda i: 3 - i)


def turned(value):
    return swapped(value, LINE, 16, lambda i: i % 4 * 4 + i // 4)


def spread_to_all(value, axis, size):
    copies = jnp.broadcast_to(value[None], (size,) + value.shape)
    return lax.all_to_all(copies, axis, 0, 0, tiled=True)


def attend(queries, key_values, segment_row, segment_col):
    count = queries.shape[0]
    heads = queries.shape[1] // HEAD_DIM
    keys, values = key_values[:, :HEAD_DIM], key_values[:, HEAD_DIM:]
    stacked = jnp.concatenate(
        [queries[:, h * HEAD_DIM : (h + 1) * HEAD_DIM] for h in range(heads)], axis=0
    )
    scores = dot(stacked, keys, ((1,), (1,))) * HEAD_DIM ** (-0.5)
    scores = scores.reshape(heads, count, count)
    allowed = (segment_col == segment_row) & (iota((count, count), 1) <= iota((count, count), 0))
    scores = jnp.where(allowed[None], scores, -1e30)
    highest = jnp.max(scores, axis=-1, keepdims=True)
    weights = jnp.exp(scores - highest)
    probs = (weights / jnp.sum(weights, axis=-1, keepdims=True)).astype(BF16)
    context = dot(probs.reshape(heads * count, count), values, ((1,), (0,))).astype(BF16)
    return jnp.concatenate(
        [context[h * count : (h + 1) * count] for h in range(heads)], axis=1
    )


def packed_routing(choice, weight):
    high = lax.reduce_precision(weight, 8, 7)
    packed = jnp.concatenate([choice.astype(F32), high, weight - high], axis=1)
    return jnp.pad(packed, ((0, 0), (0, 128 - packed.shape[1]))).astype(BF16)


def routing(packed, top, first, own_experts):
    tokens = packed.shape[0]
    local = packed[:, :top].astype(F32) - first.astype(F32)
    high, low = (packed[:, top * i : top * (i + 1)].astype(F32) for i in (1, 2))
    rows = own_experts * SLOTS
    expert = (iota((tokens, rows), 1) // SLOTS).astype(F32)
    slot = (iota((tokens, rows), 1) % SLOTS).astype(F32)
    named = jnp.zeros((tokens, rows), F32)
    highs = jnp.zeros((tokens, rows), F32)
    lows = jnp.zeros((tokens, rows), F32)
    for k in range(top):
        hit = local[:, k : k + 1] == expert
        named = jnp.where(hit, 1.0, named)
        highs = jnp.where(hit, high[:, k : k + 1], highs)
        lows = jnp.where(hit, low[:, k : k + 1], lows)
    earlier = (iota((tokens, tokens), 1) < iota((tokens, tokens), 0)).astype(BF16)
    ranks = dot(earlier, named.astype(BF16), ((1,), (0,)))
    taken = (named > 0.5) & (ranks == slot)
    parts = [jnp.where(taken, part, 0.0).astype(BF16) for part in (highs, lows)]
    return taken.astype(BF16), parts


def normalize(mid, gain):
    wide = mid.astype(F32)
    square = jnp.mean(wide * wide, axis=1, keepdims=True)
    return (wide * lax.rsqrt(square + epsilon) * gain).astype(BF16)


def experts_kernel(layout, rows_ref, *refs):
    count = sum(len(part) for parts in layout for part in parts)
    sources, (out_ref, gate_up, down, total, arrived) = refs[:count], refs[count:]
    copies = []
    for group, (up_parts, down_parts) in enumerate(layout):
        own = []
        for target, parts in ((gate_up, up_parts), (down, down_parts)):
            start = 0
            for size in parts:
                i = len(copies) + len(own)
                own.append(
                    pltpu.make_async_copy(
                        sources[i], target.at[group, pl.ds(start, size)], arrived.at[i]
                    )
                )
                start += size
        copies += own
    for copy in copies:
        copy.start()
    units = down.shape[1]
    position = 0
    for group, (up_parts, down_parts) in enumerate(layout):
        for _ in up_parts:
            copies[position].wait()
            position += 1
        projected = jnp.dot(rows_ref[...], gate_up[group], preferred_element_type=F32)
        gate, upper = projected[:, :units], projected[:, units:]
        activated = (gate / (1.0 + jnp.exp(-gate)) * upper).astype(BF16)
        for _ in down_parts:
            copies[position].wait()
            position += 1
        part = jnp.dot(activated, down[group], preferred_element_type=F32)
        if group == 0:
            total[...] = part
        else:
            total[...] += part
    out_ref[...] = total[...].astype(BF16)


def experts_of(rows, gate_ups, downs):
    layout = tuple(
        (tuple(a.shape[0] for a in ups), tuple(a.shape[0] for a in lows))
        for ups, lows in zip(gate_ups, downs)
    )
    operands = [a for ups, lows in zip(gate_ups, downs) for a in (*ups, *lows)]
    groups, (depth, columns), units = len(gate_ups), gate_ups[0][0].shape, downs[0][0].shape[0]
    vmem = pl.BlockSpec(memory_space=pltpu.VMEM)
    anywhere = pl.BlockSpec(memory_space=pl.ANY)
    return pl.pallas_call(
        functools.partial(experts_kernel, layout),
        out_shape=jax.ShapeDtypeStruct(rows.shape, BF16),
        in_specs=[vmem] + [anywhere] * len(operands),
        out_specs=vmem,
        scratch_shapes=[
            pltpu.VMEM((groups, depth, columns), BF16),
            pltpu.VMEM((groups, units, depth), BF16),
            pltpu.VMEM(rows.shape, F32),
            pltpu.SemaphoreType.DMA((len(operands),)),
        ],
        name="experts",
    )(rows, *operands)


def combined(returned, parts):
    high, low = parts
    return dot(high, returned, ((1,), (0,))) + dot(low, returned, ((1,), (0,)))


def layer(
    queries,
    key_values,
    hidden,
    lengths,
    page_table,
    out_weight,
    norm_gain,
    expert_choice,
    route_weight,
    gate_up,
    down,
):
    count = queries.shape[0]
    width = hidden.shape[1]
    n_zh, n_tp = lax.axis_size("zh"), lax.axis_size("tp")
    planes = lax.axis_size("y") * lax.axis_size("x")
    zh, tp = lax.axis_index("zh"), lax.axis_index("tp")
    share = width // n_tp
    top = expert_choice.shape[1]
    gate_up_own, down_own = gate_up[0], down[0]

    slices = [gate_up_own[i * share : (i + 1) * share] for i in range(4)] + [down_own]
    pair = [swap_units(value) for value in slices]

    projection = spread_to_all(out_weight.T, ("y", "x", "c"), 2 * planes)
    projection = projection.reshape(share, out_weight.shape[0])

    row = lengths[0]
    places = jnp.arange(count, dtype=I32)
    ends = jnp.cumsum(row)
    starts = ends - row
    segment = jnp.sum((ends[None, :] <= places[:, None]).astype(I32), axis=1)
    picked = segment[:, None] == jnp.arange(row.shape[0], dtype=I32)[None, :]
    offset = places - jnp.sum(jnp.where(picked, starts[None, :], 0), axis=1)

    context = attend(queries, key_values, segment[None, :], segment[:, None])
    contexts = [context]
    for j in range(1, n_zh):
        contexts.append(from_ahead(context, "zh", j, n_zh))
    contexts = jnp.stack(contexts)
    contexts = jnp.concatenate(
        [
            lax.dynamic_index_in_dim(contexts, (i - zh) % n_zh, 0, keepdims=False)
            for i in range(n_zh)
        ],
        axis=0,
    )

    hidden_own = turned(lax.dynamic_slice_in_dim(hidden, tp * share, share, 1))
    near_packed = packed_routing(expert_choice, route_weight)
    near_packed = turned(near_packed)
    far_packed = swap_groups(near_packed)

    cross = [swap_cores(value) for value in pair]
    core_gate_up = swap_cores(gate_up_own)
    core_down = swap_cores(down_own)
    gate_ups = [[gate_up_own], [core_gate_up], pair[:4], cross[:4]]
    downs = [[down_own], [core_down], pair[4:], cross[4:]]

    partial = dot(contexts, projection, ((1,), (1,))).astype(BF16)
    partial = lax.all_to_all(
        partial.reshape(n_zh, count, share), "tp", 0, 0, tiled=True
    )
    attn = jnp.sum(partial.astype(F32), axis=0)
    mid_own = (hidden_own.astype(F32) + attn).astype(BF16)
    mid_own = lax.optimization_barrier(mid_own)

    blocks = spread_to_all(mid_own, "zh", n_zh)
    near = jnp.concatenate([blocks[i] for i in range(n_zh)], axis=1)
    far = swap_groups(near)
    first = zh * planes

    def sent(mid, packed):
        selector, parts = routing(packed, top, first, planes)
        rows = dot(selector, normalize(mid, norm_gain), ((0,), (0,))).astype(BF16)
        rows = rows.reshape(planes, SLOTS, width)
        return lax.all_to_all(rows, PLANE, 0, 0, tiled=True), parts

    near_in, near_parts = sent(near, near_packed)
    far_in, far_parts = sent(far, far_packed)
    near_out = experts_of(near_in.reshape(-1, width), gate_ups, downs).reshape(near_in.shape)
    far_out = experts_of(far_in.reshape(-1, width), gate_ups, downs).reshape(far_in.shape)
    far_back = lax.all_to_all(far_out, PLANE, 0, 0, tiled=True)
    far_back, near_out = lax.optimization_barrier((far_back, near_out))
    near_back = lax.all_to_all(near_out, PLANE, 0, 0, tiled=True)

    far_moe = combined(far_back.reshape(-1, width), far_parts).astype(BF16)
    near_moe = combined(near_back.reshape(-1, width), near_parts)
    near_moe = (near_moe + swap_groups(far_moe).astype(F32)).astype(BF16)
    columns = jnp.stack([near_moe[:, i * share : (i + 1) * share] for i in range(n_zh)])
    gathered = lax.all_to_all(columns, "zh", 0, 0, tiled=True)
    moe = jnp.sum(gathered.astype(F32), axis=0)
    layer_out = turned((mid_own.astype(F32) + moe).astype(BF16))

    pages = page_table[0]
    flat_pages = pages.reshape(-1)
    pool = flat_pages.shape[0]
    page_of = segment * pages.shape[1] + offset // PAGE
    slot_page = jnp.sum(
        jnp.where(
            page_of[:, None] == jnp.arange(pool, dtype=I32)[None, :], flat_pages[None, :], 0
        ),
        axis=1,
    )
    cache_rows = slot_page * PAGE + offset % PAGE
    put = (iota((pool * PAGE, count), 0) == cache_rows[None, :]).astype(BF16)
    cache = dot(put, key_values, ((1,), (0,))).astype(BF16)
    return (layer_out, cache.reshape(pool, PAGE, key_values.shape[1]))


def solution(mesh):
    grid = Mesh(mesh.devices.reshape(4, 4, 4, 2, 4), AXES)
    placed = (
        P(REQ, "tp"),
        P(REQ, "tp"),
        P(REQ, None),
        P(REQ, None),
        P(REQ, None, None),
        P("tp", REQ),
        P(),
        P(REQ, None),
        P(REQ, None),
        P(REQ, None, "tp"),
        P(REQ, "tp", None),
    )
    return jax.shard_map(
        layer,
        mesh=grid,
        in_specs=placed,
        out_specs=(P(REQ, "tp"), P(REQ, None, "tp")),
        check_vma=False,
    )
```
